512 devices in a mesh: dx: 8 (over x, core), dy: 2 (over y_hi), band: 32 (over y_lo, z).
Axes of the slice: x: 4, y: 4 (y_hi: 2, y_lo: 2; y = y_hi * 2 + y_lo), z: 16, core: 2. Of those that a mesh axis runs over, the one named last changes fastest.
Arguments:
- orbitals: bfloat16 [128, 96, 8192], P('dx', 'dy', 'band'), may hold values from -6 to 6
- rotation: bfloat16 [2048, 2048], P('band'), may hold values from -0.125 to 0.125
- potential: float32 [4, 128, 96], P(None, 'dx', 'dy'), may hold values from -3 to 1
Outputs:
- rotated: bfloat16 [128, 96, 8192], P('dx', 'dy', 'band')
- applied: bfloat16 [128, 96, 8192], P('dx', 'dy', 'band')
The draws below stay inside these ranges and needn't reach their ends.
All inputs are finite; a program needn't handle non-finite values.
Results may differ from the reference program's by a relative error of at most 0.0049.
Values may be sent and summed in bfloat16 or wider, within the bound.
No kernel may reach another device: no remote copies, remote signals or barrier semaphores. Data moves between devices by JAX's collectives and lax.ppermute only.
A program may use at most 64 MiB of HBM per device.

```python
import jax
import jax.numpy as jnp

NB = 2048
NZ = 4
NX = 128
NY = 96


def levels(stream_key, shape, shards, low, high):
    level, own = 1.0, jax.random.fold_in(stream_key, 6)
    for dim, shards_of in shards:
        draws = jnp.exp(jax.random.uniform(jax.random.fold_in(own, dim), (shards_of,), jnp.float32, low / len(shards), high / len(shards)))
        level = level * jnp.repeat(draws, shape[dim] // shards_of).reshape([-1 if axis == dim else 1 for axis in range(len(shape))])
    return level


def centred(own_key, shape, width, bound, split=(), kind=jnp.bfloat16):
    gain = levels(own_key, shape, split, -0.22, 0.18) if split else 1.0
    entries = jax.random.normal(own_key, shape, jnp.float32) * width * gain
    return jnp.minimum(jnp.maximum(entries, -bound), bound).astype(kind)


def setup_inputs(seed: int = 0) -> dict:
    seeds = jax.random.split(jax.random.key(seed), 4)
    return {
        "orbitals": centred(seeds[0], (NX, NY, NB * NZ), 1.0, 6.0, ((0, 8), (1, 2), (2, 32))),
        "rotation": centred(seeds[1], (NB, NB), NB ** -0.5, 0.125, ((0, 32),)),
        "potential": jnp.clip(-3.0 + 4.0 * jax.random.uniform(seeds[2], (NZ, NX, NY), jnp.float32) ** levels(seeds[2], (NZ, NX, NY), ((1, 8), (2, 2)), -0.2, 0.2), -3.0, 1.0),
    }


stencil_weights = (-205.0 / 72.0, 8.0 / 5.0, -1.0 / 5.0, 8.0 / 315.0, -1.0 / 560.0)


def laplace_apply(values):
    cells_x, cells_y, bands_all, planes = values.shape
    padded = jnp.pad(values, ((4, 4), (4, 4), (0, 0), (4, 4)))
    result = 3.0 * stencil_weights[0] * values
    for distance in range(1, 5):
        weight = stencil_weights[distance]
        along_x = padded[4 + distance:4 + distance + cells_x, 4:4 + cells_y, :, 4:4 + planes] + padded[4 - distance:4 - distance + cells_x, 4:4 + cells_y, :, 4:4 + planes]
        along_y = padded[4:4 + cells_x, 4 + distance:4 + distance + cells_y, :, 4:4 + planes] + padded[4:4 + cells_x, 4 - distance:4 - distance + cells_y, :, 4:4 + planes]
        along_z = padded[4:4 + cells_x, 4:4 + cells_y, :, 4 + distance:4 + distance + planes] + padded[4:4 + cells_x, 4:4 + cells_y, :, 4 - distance:4 - distance + planes]
        result = result + weight * (along_z + along_x + along_y)
    return result


def reference(orbitals, rotation, potential):
    planes = potential.shape[0]
    cells_x, cells_y, merged = orbitals.shape
    bands_all = merged // planes
    psi = orbitals.reshape(cells_x, cells_y, bands_all, planes)
    flat = jnp.transpose(psi, (0, 1, 3, 2)).reshape(cells_x * cells_y * planes, bands_all)
    mixed = jnp.dot(flat, rotation.T, preferred_element_type=jnp.float32).astype(jnp.bfloat16)
    mixed = jnp.transpose(mixed.reshape(cells_x, cells_y, planes, bands_all), (0, 1, 3, 2))
    center = mixed.astype(jnp.float32)
    field = jnp.transpose(potential, (1, 2, 0))[:, :, None, :]
    applied = -0.5 * laplace_apply(center) + field * center
    rotated = mixed.reshape(cells_x, cells_y, merged)
    return rotated, applied.reshape(cells_x, cells_y, merged).astype(jnp.bfloat16)
```

```python
import functools

import jax
import jax.numpy as jnp
from jax import lax
from jax.experimental import pallas as pl
from jax.experimental.pallas import tpu as pltpu
from jax.sharding import PartitionSpec as P

stencil_weights = (-205.0 / 72.0, 8.0 / 5.0, -1.0 / 5.0, 8.0 / 315.0, -1.0 / 560.0)
PLANES = 4
VMEM = pl.BlockSpec(memory_space=pltpu.VMEM)
SMEM = pl.BlockSpec(memory_space=pltpu.SMEM)


def expand_kernel(rows_ref, out_ref):
    bands, width = rows_ref.shape
    spread = width * PLANES
    lane = lax.broadcasted_iota(jnp.int32, (spread, width), 0) // PLANES
    pick = (lane == lax.broadcasted_iota(jnp.int32, (spread, width), 1)).astype(jnp.bfloat16)
    tall = lax.dot_general(
        pick, rows_ref[...], (((1,), (1,)), ((), ())), preferred_element_type=jnp.float32
    ).astype(jnp.bfloat16)
    wide = bands * PLANES
    source = lax.broadcasted_iota(jnp.int32, (bands, wide), 0)
    target = lax.broadcasted_iota(jnp.int32, (bands, wide), 1) // PLANES
    full = jnp.dot(tall, (source == target).astype(jnp.bfloat16), preferred_element_type=jnp.float32)
    plane_in = lax.broadcasted_iota(jnp.int32, (spread, wide), 0) % PLANES
    plane_out = lax.broadcasted_iota(jnp.int32, (spread, wide), 1) % PLANES
    full = jnp.where(plane_in == plane_out, full, 0.0).astype(jnp.bfloat16)
    out_ref[...] = full.reshape(out_ref.shape)


def expand(rows):
    bands, total = rows.shape
    width = 128
    half = width * PLANES // 2
    return pl.pallas_call(
        expand_kernel,
        grid=(total // width,),
        in_specs=[pl.BlockSpec((bands, width), lambda i: (0, i))],
        out_specs=pl.BlockSpec((2, half, bands * PLANES), lambda i: (i, 0, 0)),
        out_shape=jax.ShapeDtypeStruct((2 * total // width, half, bands * PLANES), jnp.bfloat16),
        cost_estimate=pl.CostEstimate(flops=3 * 10**9, bytes_accessed=9 * 2**20, transcendentals=0),
        name="expand",
    )(rows)


def rotate_kernel(where_ref, psi_ref, near_ref, far_ref, keep_ref, send_ref, total_ref):
    step = pl.program_id(0)
    count = psi_ref.shape[0]
    part = None
    for k in range(count):
        for side, weights in ((0, near_ref), (1, far_ref)):
            term = jnp.dot(psi_ref[k, side], weights[0, k], preferred_element_type=jnp.float32)
            part = term if part is None else part + term

    @pl.when(step == 0)
    def _():
        total_ref[...] = part

    @pl.when(step > 0)
    def _():
        total_ref[...] += part

    @pl.when(step == pl.num_programs(0) - 1)
    def _():
        lanes = keep_ref.shape[1]
        keep_ref[...] = total_ref[:, :lanes].astype(jnp.bfloat16)
        send_ref[...] = total_ref[:, lanes:].astype(jnp.bfloat16)


def rotate(side, psi, weights):
    ring, _, points, lanes = psi.shape
    together = min(4, ring)
    block = (1, together, lanes, 2 * lanes)
    out = jax.ShapeDtypeStruct((points, lanes), jnp.bfloat16)
    return pl.pallas_call(
        rotate_kernel,
        grid_spec=pltpu.PrefetchScalarGridSpec(
            num_scalar_prefetch=1,
            grid=(ring // together,),
            in_specs=[
                pl.BlockSpec((together, 2, points, lanes), lambda i, s: (i, 0, 0, 0)),
                pl.BlockSpec(block, lambda i, s: (s[0], i, 0, 0)),
                pl.BlockSpec(block, lambda i, s: (1 - s[0], i, 0, 0)),
            ],
            out_specs=[pl.BlockSpec((points, lanes), lambda i, s: (0, 0))] * 2,
            scratch_shapes=[pltpu.VMEM((points, 2 * lanes), jnp.float32)],
        ),
        out_shape=[out, out],
        name="rotate",
    )(side, psi, weights, weights)


def edges_kernel(place_ref, keep_ref, got_ref, rotated_ref, low_ref, high_ref, side_ref):
    half = keep_ref.shape[0]
    mine = place_ref[0]
    rotated_ref[pl.ds(half * mine, half)] = keep_ref[...]
    rotated_ref[pl.ds(half * (1 - mine), half)] = got_ref[...]
    low_ref[...] = rotated_ref[:4]
    high_ref[...] = rotated_ref[2 * half - 4 :]
    cells_y = rotated_ref.shape[1]

    @pl.when(place_ref[1] == 0)
    def _():
        side_ref[...] = rotated_ref[:, cells_y - 4 :]

    @pl.when(place_ref[1] != 0)
    def _():
        side_ref[...] = rotated_ref[:, :4]


def edges(place, keep, got):
    half, cells_y, lanes = keep.shape
    shapes = [(2 * half, cells_y, lanes), (4, cells_y, lanes), (4, cells_y, lanes), (2 * half, 4, lanes)]
    return pl.pallas_call(
        edges_kernel,
        in_specs=[SMEM, VMEM, VMEM],
        out_specs=[VMEM] * 4,
        out_shape=[jax.ShapeDtypeStruct(s, jnp.bfloat16) for s in shapes],
        name="edges",
    )(place, keep, got)


def stencil_kernel(place_ref, rotated_ref, low_ref, high_ref, side_ref, field_ref, out_ref, pad_ref):
    cells_x, cells_y, lanes = rotated_ref.shape
    rows = slice(8, 8 + cells_y)
    pad_ref[4 : 4 + cells_x, rows] = rotated_ref[...].astype(jnp.float32)
    pad_ref[0:4, rows] = low_ref[...].astype(jnp.float32)
    pad_ref[4 + cells_x :, rows] = high_ref[...].astype(jnp.float32)
    beside = side_ref[...].astype(jnp.float32)
    first = place_ref[1] == 0
    pad_ref[4 : 4 + cells_x, 4:8] = jnp.where(first, 0.0, beside)
    pad_ref[4 : 4 + cells_x, 8 + cells_y : 12 + cells_y] = jnp.where(first, beside, 0.0)
    plane = lax.broadcasted_iota(jnp.int32, (cells_y, lanes), 1) % PLANES

    def row(x, carry):
        center = pad_ref[x + 4, rows]
        laplace = 3.0 * stencil_weights[0] * center
        for d in range(1, 5):
            total = pad_ref[x + 4 + d, rows] + pad_ref[x + 4 - d, rows]
            total += pad_ref[x + 4, 8 + d : 8 + d + cells_y] + pad_ref[x + 4, 8 - d : 8 - d + cells_y]
            if d < PLANES:
                total += jnp.where(plane + d < PLANES, pltpu.roll(center, lanes - d, 1), 0.0)
                total += jnp.where(plane >= d, pltpu.roll(center, d, 1), 0.0)
            laplace += stencil_weights[d] * total
        out_ref[x] = (field_ref[x] * center - 0.5 * laplace).astype(jnp.bfloat16)
        return carry

    lax.fori_loop(0, cells_x, row, 0)


def stencil(place, rotated, low, high, side, field):
    cells_x, cells_y, lanes = rotated.shape
    return pl.pallas_call(
        stencil_kernel,
        in_specs=[SMEM] + [VMEM] * 5,
        out_specs=VMEM,
        out_shape=jax.ShapeDtypeStruct(rotated.shape, jnp.bfloat16),
        scratch_shapes=[pltpu.VMEM((cells_x + 8, cells_y + 16, lanes), jnp.float32)],
        name="stencil",
    )(place, rotated, low, high, side, field)


def on_device(orbitals, rotation, potential):
    cells_x, cells_y, lanes = orbitals.shape
    half = cells_x // 2
    columns = lax.axis_size("band")
    ring = columns // 2
    mine = lax.axis_index("band") // ring
    across = [(i, (i + ring) % columns) for i in range(columns)]
    place = jnp.stack([mine, lax.axis_index("dy")]).astype(jnp.int32)

    sent = lax.dynamic_slice_in_dim(orbitals, half * (1 - mine), half, 0)
    kept = lax.dynamic_slice_in_dim(orbitals, half * mine, half, 0)
    came = lax.ppermute(sent, "band", across)
    rows = jnp.concatenate([rotation, lax.ppermute(rotation, "band", across)], axis=0)
    both = jnp.stack([kept, came]).reshape(1, 2, half * cells_y, lanes)
    groups = [list(range(ring)), list(range(ring, columns))]
    psi = lax.all_gather(both, "band", axis=0, tiled=True, axis_index_groups=groups)
    weights = expand(rows)
    weights = weights.reshape(2, ring, lanes, 2 * lanes)
    keep, send = rotate(place[:1], psi, weights)
    got = lax.ppermute(send, "band", across)
    shape = (half, cells_y, lanes)
    rotated, low, high, side = edges(place, keep.reshape(shape), got.reshape(shape))
    ends = lax.axis_size("dx") - 1
    above = lax.ppermute(high, "dx", [(i, i + 1) for i in range(ends)])
    below = lax.ppermute(low, "dx", [(i + 1, i) for i in range(ends)])
    beside = lax.ppermute(side, "dy", [(0, 1), (1, 0)])
    field = jnp.tile(jnp.transpose(potential, (1, 2, 0)), (1, 1, lanes // PLANES))
    applied = stencil(place, rotated, above, below, beside, field)
    return rotated, applied


def solution(mesh):
    return jax.shard_map(
        on_device,
        mesh=mesh,
        in_specs=(P("dx", "dy", "band"), P("band", None), P(None, "dx", "dy")),
        out_specs=(P("dx", "dy", "band"), P("dx", "dy", "band")),
        check_vma=False,
    )
```

```python
import functools

import jax
import jax.numpy as jnp
from jax import lax
from jax.experimental import pallas as pl
from jax.experimental.pallas import tpu as pltpu
from jax.sharding import PartitionSpec as P

stencil_weights = (-205.0 / 72.0, 8.0 / 5.0, -1.0 / 5.0, 8.0 / 315.0, -1.0 / 560.0)
PLANES = 4
VMEM = pl.BlockSpec(memory_space=pltpu.VMEM)
SMEM = pl.BlockSpec(memory_space=pltpu.SMEM)


def rotate_kernel(first, last, begin, count, *refs):
    place_ref, order_ref, rows_ref = refs[:3]
    blocks = refs[3 : 3 + count]
    refs = refs[3 + count :]
    if not first:
        before_ref, refs = refs[0], refs[1:]
    if first:
        levels_ref, refs = refs[0], refs[1:]
    bands = rows_ref.shape[0]
    lanes = blocks[0].shape[1]
    wide = bands * PLANES
    i = lax.broadcasted_iota(jnp.int32, (bands, wide), 0)
    spread = (i == lax.broadcasted_iota(jnp.int32, (bands, wide), 1) >> 2).astype(jnp.bfloat16)
    row = lax.broadcasted_iota(jnp.int32, (lanes, 128), 0) >> 2
    column = lax.broadcasted_iota(jnp.int32, (lanes, 128), 1)
    i = lax.broadcasted_iota(jnp.int32, (lanes, wide), 0)
    same = ((i ^ lax.broadcasted_iota(jnp.int32, (lanes, wide), 1)) & (PLANES - 1)) == 0
    total = None if first else before_ref[...]
    for k in range(count):
        block = order_ref[begin + k]
        start = pl.multiple_of((block >> 1) * 128, 128)
        pick = (row + (block & 1) * (lanes // PLANES) == column).astype(jnp.bfloat16)
        tall = lax.dot_general(
            pick,
            rows_ref[:, pl.ds(start, 128)],
            (((1,), (1,)), ((), ())),
            preferred_element_type=jnp.float32,
        ).astype(jnp.bfloat16)
        full = jnp.dot(tall, spread, preferred_element_type=jnp.float32)
        weights = jnp.where(same, full, 0.0).astype(jnp.bfloat16)
        term = jnp.dot(blocks[k][...], weights, preferred_element_type=jnp.float32)
        total = term if total is None else total + term
    if first:
        out_ref, field_ref = refs
        planes, cells_x, cells_y = levels_ref.shape
        q = lax.broadcasted_iota(jnp.int32, (planes, lanes), 1) & (PLANES - 1)
        cover = (q == lax.broadcasted_iota(jnp.int32, (planes, lanes), 0)).astype(jnp.float32)
        for x in range(cells_x):
            field_ref[x] = lax.dot_general(
                levels_ref[:, x],
                cover,
                (((0,), (0,)), ((), ())),
                precision=lax.Precision.HIGHEST,
                preferred_element_type=jnp.float32,
            )
    elif last:
        keep_ref, send_ref, keep_x_ref, send_x_ref, keep_y_ref, send_y_ref = refs
        near = total[:, :lanes].astype(jnp.bfloat16)
        far = total[:, lanes:].astype(jnp.bfloat16)
        keep_ref[...] = near
        send_ref[...] = far
        tall = keep_x_ref.shape[0]
        edge = pl.multiple_of(place_ref[0] * tall, tall)
        keep_x_ref[...] = keep_ref[pl.ds(edge, tall)]
        send_x_ref[...] = send_ref[pl.ds(edge, tall)]
        cells_x = keep_y_ref.shape[0]
        near = near.reshape(cells_x, -1, lanes)
        far = far.reshape(cells_x, -1, lanes)
        cells_y = near.shape[1]

        @pl.when(place_ref[1] == 0)
        def _():
            keep_y_ref[...] = near[:, cells_y - 4 :]
            send_y_ref[...] = far[:, cells_y - 4 :]

        @pl.when(place_ref[1] != 0)
        def _():
            keep_y_ref[...] = near[:, :4]
            send_y_ref[...] = far[:, :4]

        return
    else:
        (out_ref,) = refs
    out_ref[...] = total


def rotate(place, order, rows, begin, blocks, before, levels, cells, last):
    first = before is None
    points, lanes = blocks[0].shape
    total = jax.ShapeDtypeStruct((points, 2 * lanes), jnp.float32)
    args = [place, order, rows, *blocks]
    alias = {}
    if first:
        args.append(levels)
        out = [total, jax.ShapeDtypeStruct((*levels.shape[1:], lanes), jnp.float32)]
    else:
        args.append(before)
        if last:
            cells_x, cells_y = cells
            half = jax.ShapeDtypeStruct((points, lanes), jnp.bfloat16)
            x_edge = jax.ShapeDtypeStruct((4 * cells_y, lanes), jnp.bfloat16)
            y_edge = jax.ShapeDtypeStruct((cells_x, 4, lanes), jnp.bfloat16)
            out = [half, half, x_edge, x_edge, y_edge, y_edge]
        else:
            alias = {len(args) - 1: 0}
            out = [total]
    return pl.pallas_call(
        functools.partial(rotate_kernel, first, last, begin, len(blocks)),
        in_specs=[SMEM, SMEM] + [VMEM] * (len(args) - 2),
        out_specs=[VMEM] * len(out),
        out_shape=out,
        input_output_aliases=alias,
        cost_estimate=pl.CostEstimate(
            flops=2 * 10**8 * len(blocks), bytes_accessed=3 * 2**20, transcendentals=0
        ),
        name="rotate",
    )(*args)


def stencil_kernel(
    place_ref, keep_ref, got_ref, keep_x_ref, send_x_ref, keep_y_ref, send_y_ref, field_ref,
    rotated_ref, out_ref, pad_ref,
):
    cells_x, cells_y, lanes = rotated_ref.shape
    half = cells_x // 2
    rows = slice(8, 8 + cells_y)
    mine = place_ref[0]
    near, far = half * mine, half * (1 - mine)
    rotated_ref[pl.ds(near, half)] = keep_ref[...]
    rotated_ref[pl.ds(far, half)] = got_ref[...]
    pad_ref[pl.ds(4 + near, half), rows] = keep_ref[...].astype(jnp.float32)
    pad_ref[pl.ds(4 + far, half), rows] = got_ref[...].astype(jnp.float32)
    reach = cells_x + 4
    pad_ref[pl.ds(reach * (1 - mine), 4), rows] = keep_x_ref[...].astype(jnp.float32)
    pad_ref[pl.ds(reach * mine, 4), rows] = send_x_ref[...].astype(jnp.float32)
    keep_y = keep_y_ref[...].astype(jnp.float32)
    send_y = send_y_ref[...].astype(jnp.float32)
    first = place_ref[1] == 0
    above = slice(8 + cells_y, 12 + cells_y)
    pad_ref[pl.ds(4 + near, half), 4:8] = jnp.where(first, 0.0, keep_y)
    pad_ref[pl.ds(4 + far, half), 4:8] = jnp.where(first, 0.0, send_y)
    pad_ref[pl.ds(4 + near, half), above] = jnp.where(first, keep_y, 0.0)
    pad_ref[pl.ds(4 + far, half), above] = jnp.where(first, send_y, 0.0)
    plane = lax.broadcasted_iota(jnp.int32, (cells_y, lanes), 1) & (PLANES - 1)

    def row(x, carry):
        center = pad_ref[x + 4, rows]
        laplace = 3.0 * stencil_weights[0] * center
        for d in range(1, 5):
            total = pad_ref[x + 4 + d, rows] + pad_ref[x + 4 - d, rows]
            total += pad_ref[x + 4, 8 + d : 8 + d + cells_y] + pad_ref[x + 4, 8 - d : 8 - d + cells_y]
            if d < PLANES:
                total += jnp.where(plane + d < PLANES, pltpu.roll(center, lanes - d, 1), 0.0)
                total += jnp.where(plane >= d, pltpu.roll(center, d, 1), 0.0)
            laplace += stencil_weights[d] * total
        out_ref[x] = (field_ref[x] * center - 0.5 * laplace).astype(jnp.bfloat16)
        return carry

    lax.fori_loop(0, cells_x, row, 0)


def stencil(place, *arrays):
    half, cells_y, lanes = arrays[0].shape
    cells_x = 2 * half
    out = jax.ShapeDtypeStruct((cells_x, cells_y, lanes), jnp.bfloat16)
    return pl.pallas_call(
        stencil_kernel,
        in_specs=[SMEM] + [VMEM] * len(arrays),
        out_specs=[VMEM] * 2,
        out_shape=[out, out],
        scratch_shapes=[pltpu.VMEM((cells_x + 8, cells_y + 16, lanes), jnp.float32)],
        name="stencil",
    )(place, *arrays)


def on_device(orbitals, rotation, potential):
    cells_x, cells_y, lanes = orbitals.shape
    half = cells_x // 2
    points = half * cells_y
    columns = lax.axis_size("band")
    ring = columns // 2
    index = lax.axis_index("band")
    mine, z = index // ring, index % ring
    place = jnp.stack([mine, lax.axis_index("dy")]).astype(jnp.int32)
    across = [(i, (i + ring) % columns) for i in range(columns)]
    hops = {
        step: [(i, i // ring * ring + (i + step) % ring) for i in range(columns)]
        for step in (1, -1)
    }

    sent = lax.dynamic_slice_in_dim(orbitals, half * (1 - mine), half, 0)
    kept = lax.dynamic_slice_in_dim(orbitals, half * mine, half, 0)
    came = lax.ppermute(sent.reshape(points, lanes), "band", across)
    rows = jnp.concatenate([rotation, lax.ppermute(rotation, "band", across)], axis=0)

    blocks = [{0: kept.reshape(points, lanes)}, {0: came}]
    far = ring // 2
    for distance in range(1, far + 1):
        for side in (0, 1):
            for step in (1, -1):
                if distance < far or (step == 1) == (side == 0):
                    held = blocks[side][step * (distance - 1)]
                    blocks[side][step * distance] = lax.ppermute(held, "band", hops[step])
    steps = []
    for distance in range(far + 1):
        for side in (0, 1):
            steps += [(side, d) for d in sorted({distance, -distance}) if d in blocks[side]]
    sides = jnp.asarray([s for s, _ in steps], jnp.int32)
    offsets = jnp.asarray([d for _, d in steps], jnp.int32)
    order = ((mine + sides) % 2 * ring + (z - offsets) % ring).astype(jnp.int32)

    total, field, begin = None, None, 0
    tail = min(4, len(steps) // 2)
    cuts = [*range(8, len(steps) - tail, 8), len(steps) - tail, len(steps)]
    for end in cuts:
        group = [blocks[side][d] for side, d in steps[begin:end]]
        last = end == len(steps)
        out = rotate(place, order, rows, begin, group, total, potential, (half, cells_y), last)
        if total is None:
            total, field = out
        elif not last:
            (total,) = out
        begin = end
    keep, send, keep_x, send_x, keep_y, send_y = out

    ends = lax.axis_size("dx") - 1
    near, cross = [], []
    for x in range(ends):
        for i in range(ring):
            low, high = i, ring + i
            near += [(x * columns + high, (x + 1) * columns + high)]
            near += [((x + 1) * columns + low, x * columns + low)]
            cross += [(x * columns + high, (x + 1) * columns + low)]
            cross += [((x + 1) * columns + low, x * columns + high)]
    got = lax.ppermute(send, "band", across)
    keep_x = lax.ppermute(keep_x, ("dx", "band"), near)
    send_x = lax.ppermute(send_x, ("dx", "band"), cross)
    keep_y = lax.ppermute(keep_y, "dy", [(0, 1), (1, 0)])
    turn = [
        (y * columns + i, (1 - y) * columns + (i + ring) % columns)
        for y in range(2)
        for i in range(columns)
    ]
    send_y = lax.ppermute(send_y, ("dy", "band"), turn)
    shape = (half, cells_y, lanes)
    edge = (4, cells_y, lanes)
    rotated, applied = stencil(
        place, keep.reshape(shape), got.reshape(shape), keep_x.reshape(edge), send_x.reshape(edge),
        keep_y, send_y, field,
    )
    return rotated, applied


def solution(mesh):
    return jax.shard_map(
        on_device,
        mesh=mesh,
        in_specs=(P("dx", "dy", "band"), P("band", None), P(None, "dx", "dy")),
        out_specs=(P("dx", "dy", "band"), P("dx", "dy", "band")),
        check_vma=False,
    )
```

```python
import functools

import jax
import jax.numpy as jnp
from jax import lax
from jax.experimental import pallas as pl
from jax.experimental.pallas import tpu as pltpu
from jax.sharding import PartitionSpec as P


stencil_weights = (-205.0 / 72.0, 8.0 / 5.0, -1.0 / 5.0, 8.0 / 315.0, -1.0 / 560.0)
PLANES = 4
VMEM = pl.BlockSpec(memory_space=pltpu.VMEM)


def spread_kernel(own_ref, other_ref, out_ref):
    wide = out_ref.shape[1]
    columns = wide // PLANES
    row = lax.broadcasted_iota(jnp.int32, (2 * wide, 2 * columns), 0) >> 2
    column = lax.broadcasted_iota(jnp.int32, (2 * wide, 2 * columns), 1)
    pick = (row == column).astype(jnp.bfloat16)
    for pair in range(out_ref.shape[0] // 2):
        lanes = slice(2 * columns * pair, 2 * columns * (pair + 1))
        rows = jnp.concatenate([own_ref[:, lanes], other_ref[:, lanes]], axis=0)
        tall = lax.dot_general(
            pick, rows, (((1,), (1,)), ((), ())), preferred_element_type=jnp.float32
        ).astype(jnp.bfloat16)
        out_ref[2 * pair] = tall[:wide]
        out_ref[2 * pair + 1] = tall[wide:]


def spread(own, other):
    bands, total = own.shape
    return pl.pallas_call(
        spread_kernel,
        in_specs=[VMEM, VMEM],
        out_specs=VMEM,
        out_shape=jax.ShapeDtypeStruct((total // 64, 64 * PLANES, 2 * bands), jnp.bfloat16),
        cost_estimate=pl.CostEstimate(flops=5 * 10**8, bytes_accessed=3 * 2**20, transcendentals=0),
        name="spread",
    )(own, other)


def half_of_band():
    return lax.axis_size("band") // 2


def rotate_kernel(first, last, steps, *refs):
    count = len(steps)
    tall_ref = refs[0]
    shards = refs[1 : 1 + count]
    extra_ref, *refs = refs[1 + count :]
    ring = half_of_band()
    index = lax.axis_index("band")
    mine, z = index // ring, index % ring
    sign = 1 - 2 * (lax.axis_index("dx") % 2)
    second = lax.axis_index("dy")
    if last:
        sort_ref, *refs = refs
    _, _, lanes = shards[0].shape
    bands = tall_ref.shape[2]
    plane = lax.broadcasted_iota(jnp.int32, (lanes, bands), 0) & (PLANES - 1)
    masks = [(plane == q).astype(jnp.bfloat16) for q in range(PLANES)]
    left, right = [], []
    for k in range(count):
        origin = lax.rem(z - sign * steps[k] + ring, ring)
        for side in range(2):
            tall = tall_ref[(mine if side == 0 else 1 - mine) * ring + origin]
            left.append(shards[k][side])
            right.append(jnp.concatenate([tall * mask for mask in masks], axis=1))
    total = jnp.dot(
        jnp.concatenate(left, axis=1),
        jnp.concatenate(right, axis=0),
        preferred_element_type=jnp.float32,
    )
    wide = PLANES * bands
    if first:
        out_ref, field_ref, sort_ref = refs
        planes, cells_x, cells_y = extra_ref.shape
        q = lax.broadcasted_iota(jnp.int32, (planes, lanes), 1) & (PLANES - 1)
        cover = (q == lax.broadcasted_iota(jnp.int32, (planes, lanes), 0)).astype(jnp.float32)
        for x in range(cells_x):
            field_ref[x] = lax.dot_general(
                extra_ref[:, x],
                cover,
                (((0,), (0,)), ((), ())),
                precision=lax.Precision.HIGHEST,
                preferred_element_type=jnp.float32,
            )
        i = lax.broadcasted_iota(jnp.int32, (wide, wide), 0)
        j = lax.broadcasted_iota(jnp.int32, (wide, wide), 1)
        shift = bands.bit_length() - 1
        sort_ref[...] = (((i & (bands - 1)) << 2) + (i >> shift) == j).astype(jnp.bfloat16)
        out_ref[...] = total
        return
    total = total + extra_ref[...]
    if not last:
        refs[0][...] = total
        return
    keep_ref, send_ref, keep_x_ref, send_x_ref, keep_y_ref, send_y_ref = refs
    both = jnp.dot(
        total.astype(jnp.bfloat16), sort_ref[...], preferred_element_type=jnp.float32
    ).astype(jnp.bfloat16)
    near, far = both[:, :lanes], both[:, lanes:]
    keep_ref[...] = near
    send_ref[...] = far
    tall = keep_x_ref.shape[0]
    edge = pl.multiple_of(mine * tall, tall)
    keep_x_ref[...] = keep_ref[pl.ds(edge, tall)]
    send_x_ref[...] = send_ref[pl.ds(edge, tall)]
    cells_x = keep_y_ref.shape[0]
    near = near.reshape(cells_x, -1, lanes)
    far = far.reshape(cells_x, -1, lanes)
    cells_y = near.shape[1]

    @pl.when(second == 0)
    def _():
        keep_y_ref[...] = near[:, cells_y - 4 :]
        send_y_ref[...] = far[:, cells_y - 4 :]

    @pl.when(second != 0)
    def _():
        keep_y_ref[...] = near[:, :4]
        send_y_ref[...] = far[:, :4]


def rotate(tall, steps, shards, extra, sort, cells):
    first, last = 0 in steps, sort is not None
    _, points, lanes = shards[0].shape
    wide = PLANES * tall.shape[2]
    total = jax.ShapeDtypeStruct((points, wide), jnp.float32)
    args = [tall, *shards, extra]
    alias = {}
    if first:
        out = [
            total,
            jax.ShapeDtypeStruct((*extra.shape[1:], lanes), jnp.float32),
            jax.ShapeDtypeStruct((wide, wide), jnp.bfloat16),
        ]
    elif last:
        args.append(sort)
        cells_x, cells_y = cells
        half = jax.ShapeDtypeStruct((points, lanes), jnp.bfloat16)
        x_edge = jax.ShapeDtypeStruct((4 * cells_y, lanes), jnp.bfloat16)
        y_edge = jax.ShapeDtypeStruct((cells_x, 4, lanes), jnp.bfloat16)
        out = [half, half, x_edge, x_edge, y_edge, y_edge]
    else:
        alias = {len(args) - 1: 0}
        out = [total]
    return pl.pallas_call(
        functools.partial(rotate_kernel, first, last, tuple(steps)),
        in_specs=[VMEM] * len(args),
        out_specs=[VMEM] * len(out),
        out_shape=out,
        input_output_aliases=alias,
        cost_estimate=pl.CostEstimate(
            flops=4 * 10**8 * len(shards), bytes_accessed=4 * 2**20, transcendentals=0
        ),
        name="rotate",
    )(*args)


def stencil_kernel(
    keep_ref, got_ref, keep_x_ref, send_x_ref, keep_y_ref, send_y_ref, field_ref,
    rotated_ref, out_ref, pad_ref,
):
    cells_x, cells_y, lanes = rotated_ref.shape
    half = cells_x // 2
    rows = slice(8, 8 + cells_y)
    mine = lax.axis_index("band") // half_of_band()
    near, far = half * mine, half * (1 - mine)
    rotated_ref[pl.ds(near, half)] = keep_ref[...]
    rotated_ref[pl.ds(far, half)] = got_ref[...]
    pad_ref[pl.ds(4 + near, half), rows] = keep_ref[...].astype(jnp.float32)
    pad_ref[pl.ds(4 + far, half), rows] = got_ref[...].astype(jnp.float32)
    reach = cells_x + 4
    pad_ref[pl.ds(reach * (1 - mine), 4), rows] = keep_x_ref[...].astype(jnp.float32)
    pad_ref[pl.ds(reach * mine, 4), rows] = send_x_ref[...].astype(jnp.float32)
    keep_y = keep_y_ref[...].astype(jnp.float32)
    send_y = send_y_ref[...].astype(jnp.float32)
    first = lax.axis_index("dy") == 0
    above = slice(8 + cells_y, 12 + cells_y)
    pad_ref[pl.ds(4 + near, half), 4:8] = jnp.where(first, 0.0, keep_y)
    pad_ref[pl.ds(4 + far, half), 4:8] = jnp.where(first, 0.0, send_y)
    pad_ref[pl.ds(4 + near, half), above] = jnp.where(first, keep_y, 0.0)
    pad_ref[pl.ds(4 + far, half), above] = jnp.where(first, send_y, 0.0)
    plane = lax.broadcasted_iota(jnp.int32, (cells_y, lanes), 1) & (PLANES - 1)

    def row(x, carry):
        center = pad_ref[x + 4, rows]
        laplace = 3.0 * stencil_weights[0] * center
        for d in range(1, 5):
            total = pad_ref[x + 4 + d, rows] + pad_ref[x + 4 - d, rows]
            total += pad_ref[x + 4, 8 + d : 8 + d + cells_y] + pad_ref[x + 4, 8 - d : 8 - d + cells_y]
            if d < PLANES:
                total += jnp.where(plane + d < PLANES, pltpu.roll(center, lanes - d, 1), 0.0)
                total += jnp.where(plane >= d, pltpu.roll(center, d, 1), 0.0)
            laplace += stencil_weights[d] * total
        out_ref[x] = (field_ref[x] * center - 0.5 * laplace).astype(jnp.bfloat16)
        return carry

    lax.fori_loop(0, cells_x, row, 0)


def stencil(*arrays):
    half, cells_y, lanes = arrays[0].shape
    cells_x = 2 * half
    out = jax.ShapeDtypeStruct((cells_x, cells_y, lanes), jnp.bfloat16)
    return pl.pallas_call(
        stencil_kernel,
        in_specs=[VMEM] * len(arrays),
        out_specs=[VMEM] * 2,
        out_shape=[out, out],
        scratch_shapes=[pltpu.VMEM((cells_x + 8, cells_y + 16, lanes), jnp.float32)],
        name="stencil",
    )(*arrays)


def groups_of(far):
    return [[0, 1, -1]] + [[d, -d] for d in range(2, far)] + [[far]] if far > 1 else [[0], [1]]


def on_device(orbitals, rotation, potential):
    cells_x, cells_y, lanes = orbitals.shape
    half = cells_x // 2
    points = half * cells_y
    columns = lax.axis_size("band")
    ring = columns // 2
    wide = lax.axis_size("dx")
    mine = lax.axis_index("band") // ring
    across = [(i, (i + ring) % columns) for i in range(columns)]
    hops = {
        turn: [
            (x * columns + i, x * columns + i // ring * ring + (i + turn * (-1) ** x) % ring)
            for x in range(wide)
            for i in range(columns)
        ]
        for turn in (1, -1)
    }

    sent = lax.dynamic_slice_in_dim(orbitals, half * (1 - mine), half, 0)
    kept = lax.dynamic_slice_in_dim(orbitals, half * mine, half, 0)
    came = lax.ppermute(sent, "band", across)
    other = lax.ppermute(rotation, "band", across)
    tall = spread(rotation, other)

    far = ring // 2
    shards = {0: jnp.stack([kept, came]).reshape(2, points, lanes)}
    for distance in range(1, far + 1):
        for turn in (1, -1):
            if distance < far or turn == 1:
                held = shards[turn * (distance - 1)]
                shards[turn * distance] = lax.ppermute(held, ("dx", "band"), hops[turn])

    total = field = sort = None
    for group in groups_of(far):
        last = group == [far]
        out = rotate(
            tall, group, [shards[d] for d in group], potential if total is None else total,
            sort if last else None, (half, cells_y),
        )
        if total is None:
            total, field, sort = out
        elif not last:
            (total,) = out
    keep, send, keep_x, send_x, keep_y, send_y = out

    ends = lax.axis_size("dx") - 1
    near, cross = [], []
    for x in range(ends):
        for i in range(ring):
            low, high = i, ring + i
            near += [(x * columns + high, (x + 1) * columns + high)]
            near += [((x + 1) * columns + low, x * columns + low)]
            cross += [(x * columns + high, (x + 1) * columns + low)]
            cross += [((x + 1) * columns + low, x * columns + high)]
    got = lax.ppermute(send, "band", across)
    keep_x = lax.ppermute(keep_x, ("dx", "band"), near)
    send_x = lax.ppermute(send_x, ("dx", "band"), cross)
    keep_y = lax.ppermute(keep_y, "dy", [(0, 1), (1, 0)])
    turn = [
        (y * columns + i, (1 - y) * columns + (i + ring) % columns)
        for y in range(2)
        for i in range(columns)
    ]
    send_y = lax.ppermute(send_y, ("dy", "band"), turn)
    shape = (half, cells_y, lanes)
    edge = (4, cells_y, lanes)
    rotated, applied = stencil(
        keep.reshape(shape), got.reshape(shape), keep_x.reshape(edge), send_x.reshape(edge),
        keep_y, send_y, field,
    )
    return rotated, applied


def solution(mesh):
    return jax.shard_map(
        on_device,
        mesh=mesh,
        in_specs=(P("dx", "dy", "band"), P("band", None), P(None, "dx", "dy")),
        out_specs=(P("dx", "dy", "band"), P("dx", "dy", "band")),
        check_vma=False,
    )
```

```python
import functools

import jax
import jax.numpy as jnp
from jax import lax
from jax.experimental import pallas as pl
from jax.experimental.pallas import tpu as pltpu
from jax.sharding import PartitionSpec as P


stencil_weights = (-205.0 / 72.0, 8.0 / 5.0, -1.0 / 5.0, 8.0 / 315.0, -1.0 / 560.0)
PLANES = 4
VMEM = pl.BlockSpec(memory_space=pltpu.VMEM)
ANY = pl.BlockSpec(memory_space=pl.ANY)


def half_of_band():
    return lax.axis_size("band") // 2


def spread_kernel(own_ref, other_ref, out_ref, sort_ref):
    wide, double = out_ref.shape[2:]
    columns = wide // PLANES
    ring = half_of_band()
    mine = lax.axis_index("band") // ring
    row = lax.broadcasted_iota(jnp.int32, (2 * wide, 2 * columns), 0) >> 2
    column = lax.broadcasted_iota(jnp.int32, (2 * wide, 2 * columns), 1)
    pick = (row == column).astype(jnp.bfloat16)
    for pair in range(ring):
        lanes = slice(2 * columns * pair, 2 * columns * (pair + 1))
        rows = jnp.concatenate([own_ref[:, lanes], other_ref[:, lanes]], axis=0)
        tall = lax.dot_general(
            pick, rows, (((1,), (1,)), ((), ())), preferred_element_type=jnp.float32
        ).astype(jnp.bfloat16)
        for k in range(2):
            block = 2 * pair + k
            side = jnp.where(mine == block // ring, 0, 1)
            out_ref[side, block % ring] = tall[k * wide : (k + 1) * wide]
    total = PLANES * double
    i = lax.broadcasted_iota(jnp.int32, (total, total), 0)
    j = lax.broadcasted_iota(jnp.int32, (total, total), 1)
    shift = double.bit_length() - 1
    sort_ref[...] = (((i & (double - 1)) << 2) + (i >> shift) == j).astype(jnp.bfloat16)


def spread(own, other):
    bands, total = own.shape
    wide = bands * PLANES
    return pl.pallas_call(
        spread_kernel,
        in_specs=[VMEM] * 2,
        out_specs=[VMEM] * 2,
        out_shape=[
            jax.ShapeDtypeStruct((2, total // bands // 2, wide, 2 * bands), jnp.bfloat16),
            jax.ShapeDtypeStruct((2 * wide, 2 * wide), jnp.bfloat16),
        ],
        cost_estimate=pl.CostEstimate(flops=5 * 10**8, bytes_accessed=3 * 2**20, transcendentals=0),
        name="spread",
    )(own, other)


def rotate_kernel(
    tall_hbm, psi_hbm, sort_ref,
    keep_ref, send_ref, keep_x_ref, send_x_ref, keep_y_ref, send_y_ref,
    tall_ref, psi_ref, total_ref, tall_sem, psi_sem,
):
    count = psi_ref.shape[0]
    copies = []
    for k in range(count):
        copies.append(
            (
                pltpu.make_async_copy(tall_hbm.at[:, k], tall_ref.at[:, k], tall_sem.at[k]),
                pltpu.make_async_copy(psi_hbm.at[k], psi_ref.at[k], psi_sem.at[k]),
            )
        )
        for copy in copies[-1]:
            copy.start()
    lanes, bands = tall_ref.shape[2:]
    plane = lax.broadcasted_iota(jnp.int32, (lanes, bands), 0) & (PLANES - 1)
    masks = [(plane == q).astype(jnp.bfloat16) for q in range(PLANES)]
    for start in range(0, count, 4):
        group = range(start, min(count, start + 4))
        left, right = [], []
        for k in group:
            for copy in copies[k]:
                copy.wait()
            for side in range(2):
                left.append(psi_ref[k, side])
                tall = tall_ref[side, k]
                right.append(jnp.concatenate([tall * mask for mask in masks], axis=1))
        part = jnp.dot(
            jnp.concatenate(left, axis=1),
            jnp.concatenate(right, axis=0),
            preferred_element_type=jnp.float32,
        )
        if start:
            total_ref[...] += part
        else:
            total_ref[...] = part
    both = jnp.dot(
        total_ref[...].astype(jnp.bfloat16), sort_ref[...], preferred_element_type=jnp.float32
    ).astype(jnp.bfloat16)
    near, far = both[:, :lanes], both[:, lanes:]
    keep_ref[...] = near
    send_ref[...] = far
    tall = keep_x_ref.shape[0]
    mine = lax.axis_index("band") // half_of_band()
    edge = pl.multiple_of(mine * tall, tall)
    keep_x_ref[...] = keep_ref[pl.ds(edge, tall)]
    send_x_ref[...] = send_ref[pl.ds(edge, tall)]
    cells_x = keep_y_ref.shape[0]
    near = near.reshape(cells_x, -1, lanes)
    far = far.reshape(cells_x, -1, lanes)
    cells_y = near.shape[1]
    second = lax.axis_index("dy")

    @pl.when(second == 0)
    def _():
        keep_y_ref[...] = near[:, cells_y - 4 :]
        send_y_ref[...] = far[:, cells_y - 4 :]

    @pl.when(second != 0)
    def _():
        keep_y_ref[...] = near[:, :4]
        send_y_ref[...] = far[:, :4]


def rotate(tall, psi, sort, cells):
    count, _, points, lanes = psi.shape
    total = (points, PLANES * tall.shape[3])
    cells_x, cells_y = cells
    half = jax.ShapeDtypeStruct((points, lanes), jnp.bfloat16)
    x_edge = jax.ShapeDtypeStruct((4 * cells_y, lanes), jnp.bfloat16)
    y_edge = jax.ShapeDtypeStruct((cells_x, 4, lanes), jnp.bfloat16)
    return pl.pallas_call(
        rotate_kernel,
        in_specs=[ANY, ANY, VMEM],
        out_specs=[VMEM] * 6,
        out_shape=[half, half, x_edge, x_edge, y_edge, y_edge],
        scratch_shapes=[
            pltpu.VMEM(tall.shape, jnp.bfloat16),
            pltpu.VMEM(psi.shape, jnp.bfloat16),
            pltpu.VMEM(total, jnp.float32),
            pltpu.SemaphoreType.DMA((count,)),
            pltpu.SemaphoreType.DMA((count,)),
        ],
        name="rotate",
    )(tall, psi, sort)


def stencil_kernel(
    keep_ref, got_ref, keep_x_ref, send_x_ref, keep_y_ref, send_y_ref, levels_ref,
    rotated_ref, out_ref, pad_ref,
):
    cells_x, cells_y, lanes = rotated_ref.shape
    half = cells_x // 2
    rows = slice(8, 8 + cells_y)
    mine = lax.axis_index("band") // half_of_band()
    near, far = half * mine, half * (1 - mine)
    rotated_ref[pl.ds(near, half)] = keep_ref[...]
    rotated_ref[pl.ds(far, half)] = got_ref[...]
    pad_ref[pl.ds(4 + near, half), rows] = keep_ref[...].astype(jnp.float32)
    pad_ref[pl.ds(4 + far, half), rows] = got_ref[...].astype(jnp.float32)
    reach = cells_x + 4
    pad_ref[pl.ds(reach * (1 - mine), 4), rows] = keep_x_ref[...].astype(jnp.float32)
    pad_ref[pl.ds(reach * mine, 4), rows] = send_x_ref[...].astype(jnp.float32)
    keep_y = keep_y_ref[...].astype(jnp.float32)
    send_y = send_y_ref[...].astype(jnp.float32)
    first = lax.axis_index("dy") == 0
    above = slice(8 + cells_y, 12 + cells_y)
    pad_ref[pl.ds(4 + near, half), 4:8] = jnp.where(first, 0.0, keep_y)
    pad_ref[pl.ds(4 + far, half), 4:8] = jnp.where(first, 0.0, send_y)
    pad_ref[pl.ds(4 + near, half), above] = jnp.where(first, keep_y, 0.0)
    pad_ref[pl.ds(4 + far, half), above] = jnp.where(first, send_y, 0.0)
    i = lax.broadcasted_iota(jnp.int32, (lanes, lanes), 0)
    j = lax.broadcasted_iota(jnp.int32, (lanes, lanes), 1)
    apart = jnp.abs(i - j)
    weights = jnp.where(apart == 0, 3.0 * stencil_weights[0], 0.0)
    for d in range(1, PLANES):
        weights = jnp.where(apart == d, stencil_weights[d], weights)
    weights = jnp.where(i // PLANES == j // PLANES, weights, 0.0)
    terms = []
    for _ in range(3):
        terms.append(weights.astype(jnp.bfloat16))
        weights = weights - terms[-1].astype(jnp.float32)
    q = lax.broadcasted_iota(jnp.int32, (PLANES, lanes), 1) & (PLANES - 1)
    cover = (q == lax.broadcasted_iota(jnp.int32, (PLANES, lanes), 0)).astype(jnp.float32)
    for x in range(cells_x):
        laplace = jnp.dot(rotated_ref[x], terms[2], preferred_element_type=jnp.float32)
        laplace += jnp.dot(rotated_ref[x], terms[1], preferred_element_type=jnp.float32)
        laplace += jnp.dot(rotated_ref[x], terms[0], preferred_element_type=jnp.float32)
        for d in range(1, 5):
            total = pad_ref[x + 4 + d, rows] + pad_ref[x + 4 - d, rows]
            total += pad_ref[x + 4, 8 + d : 8 + d + cells_y] + pad_ref[x + 4, 8 - d : 8 - d + cells_y]
            laplace += stencil_weights[d] * total
        field = lax.dot_general(
            levels_ref[:, x],
            cover,
            (((0,), (0,)), ((), ())),
            precision=lax.Precision.HIGHEST,
            preferred_element_type=jnp.float32,
        )
        out_ref[x] = (field * pad_ref[x + 4, rows] - 0.5 * laplace).astype(jnp.bfloat16)


def stencil(*arrays):
    half, cells_y, lanes = arrays[0].shape
    cells_x = 2 * half
    out = jax.ShapeDtypeStruct((cells_x, cells_y, lanes), jnp.bfloat16)
    return pl.pallas_call(
        stencil_kernel,
        in_specs=[VMEM] * len(arrays),
        out_specs=[VMEM] * 2,
        out_shape=[out, out],
        scratch_shapes=[pltpu.VMEM((cells_x + 8, cells_y + 16, lanes), jnp.float32)],
        name="stencil",
    )(*arrays)


def on_device(orbitals, rotation, potential):
    cells_x, cells_y, lanes = orbitals.shape
    half = cells_x // 2
    points = half * cells_y
    columns = lax.axis_size("band")
    ring = columns // 2
    mine = lax.axis_index("band") // ring
    across = [(i, (i + ring) % columns) for i in range(columns)]

    sent = lax.dynamic_slice_in_dim(orbitals, half * (1 - mine), half, 0)
    kept = lax.dynamic_slice_in_dim(orbitals, half * mine, half, 0)
    came = lax.ppermute(sent, "band", across)
    both = jnp.stack([kept, came]).reshape(1, 2, points, lanes)
    groups = [list(range(ring)), list(range(ring, columns))]
    psi = lax.all_gather(both, "band", axis=0, tiled=True, axis_index_groups=groups)
    tall, sort = spread(rotation, lax.ppermute(rotation, "band", across))
    out = rotate(tall, psi, sort, (half, cells_y))
    keep, send, keep_x, send_x, keep_y, send_y = out

    ends = lax.axis_size("dx") - 1
    near, cross = [], []
    for x in range(ends):
        for i in range(ring):
            low, high = i, ring + i
            near += [(x * columns + high, (x + 1) * columns + high)]
            near += [((x + 1) * columns + low, x * columns + low)]
            cross += [(x * columns + high, (x + 1) * columns + low)]
            cross += [((x + 1) * columns + low, x * columns + high)]
    got = lax.ppermute(send, "band", across)
    keep_x = lax.ppermute(keep_x, ("dx", "band"), near)
    send_x = lax.ppermute(send_x, ("dx", "band"), cross)
    keep_y = lax.ppermute(keep_y, "dy", [(0, 1), (1, 0)])
    turn = [
        (y * columns + i, (1 - y) * columns + (i + ring) % columns)
        for y in range(2)
        for i in range(columns)
    ]
    send_y = lax.ppermute(send_y, ("dy", "band"), turn)
    shape = (half, cells_y, lanes)
    edge = (4, cells_y, lanes)
    rotated, applied = stencil(
        keep.reshape(shape), got.reshape(shape), keep_x.reshape(edge), send_x.reshape(edge),
        keep_y, send_y, potential,
    )
    return rotated, applied


def solution(mesh):
    return jax.shard_map(
        on_device,
        mesh=mesh,
        in_specs=(P("dx", "dy", "band"), P("band", None), P(None, "dx", "dy")),
        out_specs=(P("dx", "dy", "band"), P("dx", "dy", "band")),
        check_vma=False,
    )
```

```python
import jax
import jax.numpy as jnp
from jax import lax
from jax.experimental import pallas as pl
from jax.experimental.pallas import tpu as pltpu
from jax.sharding import PartitionSpec as P


stencil_weights = (-205.0 / 72.0, 8.0 / 5.0, -1.0 / 5.0, 8.0 / 315.0, -1.0 / 560.0)
PLANES = 4
VMEM = pl.BlockSpec(memory_space=pltpu.VMEM)
ANY = pl.BlockSpec(memory_space=pl.ANY)


def half_of_band():
    return lax.axis_size("band") // 2


def spread_kernel(own_ref, other_ref, out_ref):
    wide = out_ref.shape[2]
    columns = wide // PLANES
    ring = half_of_band()
    mine = lax.axis_index("band") // ring
    row = lax.broadcasted_iota(jnp.int32, (2 * wide, 2 * columns), 0) >> 2
    column = lax.broadcasted_iota(jnp.int32, (2 * wide, 2 * columns), 1)
    pick = (row == column).astype(jnp.bfloat16)
    for pair in range(ring):
        lanes = slice(2 * columns * pair, 2 * columns * (pair + 1))
        rows = jnp.concatenate([own_ref[:, lanes], other_ref[:, lanes]], axis=0)
        tall = lax.dot_general(
            pick, rows, (((1,), (1,)), ((), ())), preferred_element_type=jnp.float32
        ).astype(jnp.bfloat16)
        for k in range(2):
            block = 2 * pair + k
            side = jnp.where(mine == block // ring, 0, 1)
            out_ref[side, block % ring] = tall[k * wide : (k + 1) * wide]


def spread(own, other):
    bands, total = own.shape
    wide = bands * PLANES
    return pl.pallas_call(
        spread_kernel,
        in_specs=[VMEM] * 2,
        out_specs=VMEM,
        out_shape=jax.ShapeDtypeStruct((2, total // bands // 2, wide, 2 * bands), jnp.bfloat16),
        cost_estimate=pl.CostEstimate(flops=5 * 10**8, bytes_accessed=3 * 2**20, transcendentals=0),
        name="spread",
    )(own, other)


def rotate_kernel(
    tall_hbm, psi_hbm,
    keep_ref, send_ref, keep_x_ref, send_x_ref, keep_y_ref, send_y_ref,
    tall_ref, psi_ref, total_ref, sort_ref, tall_sem, psi_sem,
):
    count = psi_ref.shape[0]
    copies = []
    for k in range(count):
        copies.append(
            (
                pltpu.make_async_copy(tall_hbm.at[:, k], tall_ref.at[:, k], tall_sem.at[k]),
                pltpu.make_async_copy(psi_hbm.at[k], psi_ref.at[k], psi_sem.at[k]),
            )
        )
        for copy in copies[-1]:
            copy.start()
    lanes, bands = tall_ref.shape[2:]
    i = lax.broadcasted_iota(jnp.int32, sort_ref.shape, 0)
    j = lax.broadcasted_iota(jnp.int32, sort_ref.shape, 1)
    shift = bands.bit_length() - 1
    sort_ref[...] = (((i & (bands - 1)) << 2) + (i >> shift) == j).astype(jnp.bfloat16)
    plane = lax.broadcasted_iota(jnp.int32, (lanes, bands), 0) & (PLANES - 1)
    masks = [(plane == q).astype(jnp.bfloat16) for q in range(PLANES)]
    for k in range(count):
        for copy in copies[k]:
            copy.wait()
        weights = []
        for side in range(2):
            tall = tall_ref[side, k]
            weights.append(jnp.concatenate([tall * mask for mask in masks], axis=1))
        part = jnp.dot(
            jnp.concatenate([psi_ref[k, 0], psi_ref[k, 1]], axis=1),
            jnp.concatenate(weights, axis=0),
            preferred_element_type=jnp.float32,
        )
        if k:
            total_ref[...] += part
        else:
            total_ref[...] = part
    both = jnp.dot(
        total_ref[...].astype(jnp.bfloat16), sort_ref[...], preferred_element_type=jnp.float32
    ).astype(jnp.bfloat16)
    near, far = both[:, :lanes], both[:, lanes:]
    keep_ref[...] = near
    send_ref[...] = far
    tall = keep_x_ref.shape[0]
    mine = lax.axis_index("band") // half_of_band()
    edge = pl.multiple_of(mine * tall, tall)
    keep_x_ref[...] = keep_ref[pl.ds(edge, tall)]
    send_x_ref[...] = send_ref[pl.ds(edge, tall)]
    cells_x = keep_y_ref.shape[0]
    near = near.reshape(cells_x, -1, lanes)
    far = far.reshape(cells_x, -1, lanes)
    cells_y = near.shape[1]
    second = lax.axis_index("dy")

    @pl.when(second == 0)
    def _():
        keep_y_ref[...] = near[:, cells_y - 4 :]
        send_y_ref[...] = far[:, cells_y - 4 :]

    @pl.when(second != 0)
    def _():
        keep_y_ref[...] = near[:, :4]
        send_y_ref[...] = far[:, :4]


def rotate(tall, psi, cells):
    count, _, points, lanes = psi.shape
    total = (points, PLANES * tall.shape[3])
    cells_x, cells_y = cells
    half = jax.ShapeDtypeStruct((points, lanes), jnp.bfloat16)
    x_edge = jax.ShapeDtypeStruct((4 * cells_y, lanes), jnp.bfloat16)
    y_edge = jax.ShapeDtypeStruct((cells_x, 4, lanes), jnp.bfloat16)
    return pl.pallas_call(
        rotate_kernel,
        in_specs=[ANY, ANY],
        out_specs=[VMEM] * 6,
        out_shape=[half, half, x_edge, x_edge, y_edge, y_edge],
        scratch_shapes=[
            pltpu.VMEM(tall.shape, jnp.bfloat16),
            pltpu.VMEM(psi.shape, jnp.bfloat16),
            pltpu.VMEM(total, jnp.float32),
            pltpu.VMEM((total[1], total[1]), jnp.bfloat16),
            pltpu.SemaphoreType.DMA((count,)),
            pltpu.SemaphoreType.DMA((count,)),
        ],
        name="rotate",
    )(tall, psi)


def stencil_kernel(
    keep_ref, got_ref, keep_x_ref, send_x_ref, keep_y_ref, send_y_ref, levels_ref,
    rotated_ref, out_ref, pad_ref,
):
    cells_x, cells_y, lanes = rotated_ref.shape
    half = cells_x // 2
    rows = slice(8, 8 + cells_y)
    mine = lax.axis_index("band") // half_of_band()
    near, far = half * mine, half * (1 - mine)
    rotated_ref[pl.ds(near, half)] = keep_ref[...]
    rotated_ref[pl.ds(far, half)] = got_ref[...]
    pad_ref[pl.ds(4 + near, half), rows] = keep_ref[...].astype(jnp.float32)
    pad_ref[pl.ds(4 + far, half), rows] = got_ref[...].astype(jnp.float32)
    reach = cells_x + 4
    pad_ref[pl.ds(reach * (1 - mine), 4), rows] = keep_x_ref[...].astype(jnp.float32)
    pad_ref[pl.ds(reach * mine, 4), rows] = send_x_ref[...].astype(jnp.float32)
    keep_y = keep_y_ref[...].astype(jnp.float32)
    send_y = send_y_ref[...].astype(jnp.float32)
    first = lax.axis_index("dy") == 0
    above = slice(8 + cells_y, 12 + cells_y)
    pad_ref[pl.ds(4 + near, half), 4:8] = jnp.where(first, 0.0, keep_y)
    pad_ref[pl.ds(4 + far, half), 4:8] = jnp.where(first, 0.0, send_y)
    pad_ref[pl.ds(4 + near, half), above] = jnp.where(first, keep_y, 0.0)
    pad_ref[pl.ds(4 + far, half), above] = jnp.where(first, send_y, 0.0)
    i = lax.broadcasted_iota(jnp.int32, (lanes, lanes), 0)
    j = lax.broadcasted_iota(jnp.int32, (lanes, lanes), 1)
    apart = jnp.abs(i - j)
    weights = jnp.where(apart == 0, 3.0 * stencil_weights[0], 0.0)
    for d in range(1, PLANES):
        weights = jnp.where(apart == d, stencil_weights[d], weights)
    weights = jnp.where(i // PLANES == j // PLANES, weights, 0.0)
    terms = []
    for _ in range(3):
        terms.append(weights.astype(jnp.bfloat16))
        weights = weights - terms[-1].astype(jnp.float32)
    q = lax.broadcasted_iota(jnp.int32, (PLANES, lanes), 1) & (PLANES - 1)
    cover = (q == lax.broadcasted_iota(jnp.int32, (PLANES, lanes), 0)).astype(jnp.float32)
    for x in range(cells_x):
        laplace = jnp.dot(rotated_ref[x], terms[2], preferred_element_type=jnp.float32)
        laplace += jnp.dot(rotated_ref[x], terms[1], preferred_element_type=jnp.float32)
        laplace += jnp.dot(rotated_ref[x], terms[0], preferred_element_type=jnp.float32)
        for d in range(1, 5):
            total = pad_ref[x + 4 + d, rows] + pad_ref[x + 4 - d, rows]
            total += pad_ref[x + 4, 8 + d : 8 + d + cells_y] + pad_ref[x + 4, 8 - d : 8 - d + cells_y]
            laplace += stencil_weights[d] * total
        field = lax.dot_general(
            levels_ref[:, x],
            cover,
            (((0,), (0,)), ((), ())),
            precision=lax.Precision.HIGHEST,
            preferred_element_type=jnp.float32,
        )
        out_ref[x] = (field * pad_ref[x + 4, rows] - 0.5 * laplace).astype(jnp.bfloat16)


def stencil(*arrays):
    half, cells_y, lanes = arrays[0].shape
    cells_x = 2 * half
    out = jax.ShapeDtypeStruct((cells_x, cells_y, lanes), jnp.bfloat16)
    return pl.pallas_call(
        stencil_kernel,
        in_specs=[VMEM] * len(arrays),
        out_specs=[VMEM] * 2,
        out_shape=[out, out],
        scratch_shapes=[pltpu.VMEM((cells_x + 8, cells_y + 16, lanes), jnp.float32)],
        name="stencil",
    )(*arrays)


def on_device(orbitals, rotation, potential):
    cells_x, cells_y, lanes = orbitals.shape
    half = cells_x // 2
    points = half * cells_y
    columns = lax.axis_size("band")
    ring = columns // 2
    mine = lax.axis_index("band") // ring
    across = [(i, (i + ring) % columns) for i in range(columns)]

    sent = lax.dynamic_slice_in_dim(orbitals, half * (1 - mine), half, 0)
    kept = lax.dynamic_slice_in_dim(orbitals, half * mine, half, 0)
    came = lax.ppermute(sent, "band", across)
    both = jnp.stack([kept, came]).reshape(1, 2, points, lanes)
    groups = [list(range(ring)), list(range(ring, columns))]
    psi = lax.all_gather(both, "band", axis=0, tiled=True, axis_index_groups=groups)
    tall = spread(rotation, lax.ppermute(rotation, "band", across))
    out = rotate(tall, psi, (half, cells_y))
    keep, send, keep_x, send_x, keep_y, send_y = out

    ends = lax.axis_size("dx") - 1
    near, cross = [], []
    for x in range(ends):
        for i in range(ring):
            low, high = i, ring + i
            near += [(x * columns + high, (x + 1) * columns + high)]
            near += [((x + 1) * columns + low, x * columns + low)]
            cross += [(x * columns + high, (x + 1) * columns + low)]
            cross += [((x + 1) * columns + low, x * columns + high)]
    turn = [
        (y * columns + i, (1 - y) * columns + (i + ring) % columns)
        for y in range(2)
        for i in range(columns)
    ]
    keep_y = lax.ppermute(keep_y, "dy", [(0, 1), (1, 0)])
    send_y = lax.ppermute(send_y, ("dy", "band"), turn)
    got = lax.ppermute(send, "band", across)
    keep_x = lax.ppermute(keep_x, ("dx", "band"), near)
    send_x = lax.ppermute(send_x, ("dx", "band"), cross)
    shape = (half, cells_y, lanes)
    edge = (4, cells_y, lanes)
    rotated, applied = stencil(
        keep.reshape(shape), got.reshape(shape), keep_x.reshape(edge), send_x.reshape(edge),
        keep_y, send_y, potential,
    )
    return rotated, applied


def solution(mesh):
    return jax.shard_map(
        on_device,
        mesh=mesh,
        in_specs=(P("dx", "dy", "band"), P("band", None), P(None, "dx", "dy")),
        out_specs=(P("dx", "dy", "band"), P("dx", "dy", "band")),
        check_vma=False,
    )
```

```python
import jax
import jax.numpy as jnp
from jax import lax
from jax.experimental import pallas as pl
from jax.experimental.pallas import tpu as pltpu
from jax.sharding import PartitionSpec as P


stencil_weights = (-205.0 / 72.0, 8.0 / 5.0, -1.0 / 5.0, 8.0 / 315.0, -1.0 / 560.0)
PLANES = 4
VMEM = pl.BlockSpec(memory_space=pltpu.VMEM)
ANY = pl.BlockSpec(memory_space=pl.ANY)
HBM = pl.BlockSpec(memory_space=pltpu.HBM)


def half_of_band():
    return lax.axis_size("band") // 2


def spread_kernel(own_ref, other_ref, out_ref):
    wide = out_ref.shape[2]
    columns = wide // PLANES
    ring = half_of_band()
    mine = lax.axis_index("band") // ring
    row = lax.broadcasted_iota(jnp.int32, (2 * wide, 2 * columns), 0) >> 2
    column = lax.broadcasted_iota(jnp.int32, (2 * wide, 2 * columns), 1)
    pick = (row == column).astype(jnp.bfloat16)
    for pair in range(ring):
        lanes = slice(2 * columns * pair, 2 * columns * (pair + 1))
        rows = jnp.concatenate([own_ref[:, lanes], other_ref[:, lanes]], axis=0)
        tall = lax.dot_general(
            pick, rows, (((1,), (1,)), ((), ())), preferred_element_type=jnp.float32
        ).astype(jnp.bfloat16)
        for k in range(2):
            block = 2 * pair + k
            side = jnp.where(mine == block // ring, 0, 1)
            out_ref[side, block % ring] = tall[k * wide : (k + 1) * wide]


def spread(own, other):
    bands, total = own.shape
    wide = bands * PLANES
    return pl.pallas_call(
        spread_kernel,
        in_specs=[VMEM] * 2,
        out_specs=VMEM,
        out_shape=jax.ShapeDtypeStruct((2, total // bands // 2, wide, 2 * bands), jnp.bfloat16),
        cost_estimate=pl.CostEstimate(flops=5 * 10**8, bytes_accessed=3 * 2**20, transcendentals=0),
        compiler_params=pltpu.CompilerParams(vmem_limit_bytes=12 * 2**20),
        name="spread",
    )(own, other)


def rotate_kernel(
    tall_hbm, psi_hbm,
    keep_ref, send_ref, keep_x_ref, send_x_ref, keep_y_ref, send_y_ref,
    tall_ref, psi_ref, total_ref, sort_ref, tall_sem, psi_sem,
):
    count = psi_ref.shape[0]
    copies = []
    for k in range(count):
        copies.append(
            (
                pltpu.make_async_copy(tall_hbm.at[:, k], tall_ref.at[:, k], tall_sem.at[k]),
                pltpu.make_async_copy(psi_hbm.at[k], psi_ref.at[k], psi_sem.at[k]),
            )
        )
        for copy in copies[-1]:
            copy.start()
    lanes, bands = tall_ref.shape[2:]
    i = lax.broadcasted_iota(jnp.int32, sort_ref.shape, 0)
    j = lax.broadcasted_iota(jnp.int32, sort_ref.shape, 1)
    shift = bands.bit_length() - 1
    sort_ref[...] = (((i & (bands - 1)) << 2) + (i >> shift) == j).astype(jnp.bfloat16)
    plane = lax.broadcasted_iota(jnp.int32, (lanes, bands), 0) & (PLANES - 1)
    masks = [(plane == q).astype(jnp.bfloat16) for q in range(PLANES)]
    for k in range(count):
        for copy in copies[k]:
            copy.wait()
        weights = []
        for side in range(2):
            tall = tall_ref[side, k]
            weights.append(jnp.concatenate([tall * mask for mask in masks], axis=1))
        part = jnp.dot(
            jnp.concatenate([psi_ref[k, 0], psi_ref[k, 1]], axis=1),
            jnp.concatenate(weights, axis=0),
            preferred_element_type=jnp.float32,
        )
        if k:
            total_ref[...] += part
        else:
            total_ref[...] = part
    both = jnp.dot(
        total_ref[...].astype(jnp.bfloat16), sort_ref[...], preferred_element_type=jnp.float32
    ).astype(jnp.bfloat16)
    near, far = both[:, :lanes], both[:, lanes:]
    keep_ref[...] = near
    send_ref[...] = far
    tall = keep_x_ref.shape[0]
    mine = lax.axis_index("band") // half_of_band()
    edge = pl.multiple_of(mine * tall, tall)
    keep_x_ref[...] = keep_ref[pl.ds(edge, tall)]
    send_x_ref[...] = send_ref[pl.ds(edge, tall)]
    cells_x = keep_y_ref.shape[0]
    near = near.reshape(cells_x, -1, lanes)
    far = far.reshape(cells_x, -1, lanes)
    cells_y = near.shape[1]
    second = lax.axis_index("dy")

    @pl.when(second == 0)
    def _():
        keep_y_ref[...] = near[:, cells_y - 4 :]
        send_y_ref[...] = far[:, cells_y - 4 :]

    @pl.when(second != 0)
    def _():
        keep_y_ref[...] = near[:, :4]
        send_y_ref[...] = far[:, :4]


def rotate(tall, psi, cells):
    count, _, points, lanes = psi.shape
    total = (points, PLANES * tall.shape[3])
    cells_x, cells_y = cells
    half = jax.ShapeDtypeStruct((points, lanes), jnp.bfloat16)
    x_edge = jax.ShapeDtypeStruct((4 * cells_y, lanes), jnp.bfloat16)
    y_edge = jax.ShapeDtypeStruct((cells_x, 4, lanes), jnp.bfloat16)
    return pl.pallas_call(
        rotate_kernel,
        in_specs=[ANY, HBM],
        out_specs=[VMEM] * 6,
        out_shape=[half, half, x_edge, x_edge, y_edge, y_edge],
        scratch_shapes=[
            pltpu.VMEM(tall.shape, jnp.bfloat16),
            pltpu.VMEM(psi.shape, jnp.bfloat16),
            pltpu.VMEM(total, jnp.float32),
            pltpu.VMEM((total[1], total[1]), jnp.bfloat16),
            pltpu.SemaphoreType.DMA((count,)),
            pltpu.SemaphoreType.DMA((count,)),
        ],
        compiler_params=pltpu.CompilerParams(vmem_limit_bytes=49 * 2**20),
        name="rotate",
    )(tall, psi)


def stencil_kernel(
    keep_hbm, got_hbm, keep_x_hbm, send_x_hbm, keep_y_hbm, send_y_hbm, levels_hbm,
    rotated_ref, out_ref, pad_ref, keep_ref, got_ref, keep_x_ref, send_x_ref, keep_y_ref, send_y_ref, levels_ref,
    sem,
):
    sources = [keep_hbm, got_hbm, keep_x_hbm, send_x_hbm, keep_y_hbm, send_y_hbm, levels_hbm]
    targets = [keep_ref, got_ref, keep_x_ref, send_x_ref, keep_y_ref, send_y_ref, levels_ref]
    copies = [
        pltpu.make_async_copy(source, target, sem.at[k])
        for k, (source, target) in enumerate(zip(sources, targets))
    ]
    for copy in copies:
        copy.start()
    for copy in copies:
        copy.wait()
    cells_x, cells_y, lanes = rotated_ref.shape
    half = cells_x // 2
    rows = slice(8, 8 + cells_y)
    mine = lax.axis_index("band") // half_of_band()
    near, far = half * mine, half * (1 - mine)
    rotated_ref[pl.ds(near, half)] = keep_ref[...]
    rotated_ref[pl.ds(far, half)] = got_ref[...]
    pad_ref[pl.ds(4 + near, half), rows] = keep_ref[...].astype(jnp.float32)
    pad_ref[pl.ds(4 + far, half), rows] = got_ref[...].astype(jnp.float32)
    reach = cells_x + 4
    pad_ref[pl.ds(reach * (1 - mine), 4), rows] = keep_x_ref[...].astype(jnp.float32)
    pad_ref[pl.ds(reach * mine, 4), rows] = send_x_ref[...].astype(jnp.float32)
    keep_y = keep_y_ref[...].astype(jnp.float32)
    send_y = send_y_ref[...].astype(jnp.float32)
    first = lax.axis_index("dy") == 0
    above = slice(8 + cells_y, 12 + cells_y)
    pad_ref[pl.ds(4 + near, half), 4:8] = jnp.where(first, 0.0, keep_y)
    pad_ref[pl.ds(4 + far, half), 4:8] = jnp.where(first, 0.0, send_y)
    pad_ref[pl.ds(4 + near, half), above] = jnp.where(first, keep_y, 0.0)
    pad_ref[pl.ds(4 + far, half), above] = jnp.where(first, send_y, 0.0)
    i = lax.broadcasted_iota(jnp.int32, (lanes, lanes), 0)
    j = lax.broadcasted_iota(jnp.int32, (lanes, lanes), 1)
    apart = jnp.abs(i - j)
    weights = jnp.where(apart == 0, 3.0 * stencil_weights[0], 0.0)
    for d in range(1, PLANES):
        weights = jnp.where(apart == d, stencil_weights[d], weights)
    weights = jnp.where(i // PLANES == j // PLANES, weights, 0.0)
    terms = []
    for _ in range(3):
        terms.append(weights.astype(jnp.bfloat16))
        weights = weights - terms[-1].astype(jnp.float32)
    q = lax.broadcasted_iota(jnp.int32, (PLANES, lanes), 1) & (PLANES - 1)
    cover = (q == lax.broadcasted_iota(jnp.int32, (PLANES, lanes), 0)).astype(jnp.float32)
    for x in range(cells_x):
        laplace = jnp.dot(rotated_ref[x], terms[2], preferred_element_type=jnp.float32)
        laplace += jnp.dot(rotated_ref[x], terms[1], preferred_element_type=jnp.float32)
        laplace += jnp.dot(rotated_ref[x], terms[0], preferred_element_type=jnp.float32)
        for d in range(1, 5):
            total = pad_ref[x + 4 + d, rows] + pad_ref[x + 4 - d, rows]
            total += pad_ref[x + 4, 8 + d : 8 + d + cells_y] + pad_ref[x + 4, 8 - d : 8 - d + cells_y]
            laplace += stencil_weights[d] * total
        field = lax.dot_general(
            levels_ref[:, x],
            cover,
            (((0,), (0,)), ((), ())),
            precision=lax.Precision.HIGHEST,
            preferred_element_type=jnp.float32,
        )
        out_ref[x] = (field * pad_ref[x + 4, rows] - 0.5 * laplace).astype(jnp.bfloat16)


def stencil(*arrays):
    half, cells_y, lanes = arrays[0].shape
    cells_x = 2 * half
    out = jax.ShapeDtypeStruct((cells_x, cells_y, lanes), jnp.bfloat16)
    return pl.pallas_call(
        stencil_kernel,
        in_specs=[ANY] * len(arrays),
        out_specs=[VMEM] * 2,
        out_shape=[out, out],
        scratch_shapes=[
            pltpu.VMEM((cells_x + 8, cells_y + 16, lanes), jnp.float32),
            *[pltpu.VMEM(a.shape, a.dtype) for a in arrays],
            pltpu.SemaphoreType.DMA((len(arrays),)),
        ],
        compiler_params=pltpu.CompilerParams(vmem_limit_bytes=12 * 2**20),
        name="stencil",
    )(*arrays)


def on_device(orbitals, rotation, potential):
    cells_x, cells_y, lanes = orbitals.shape
    half = cells_x // 2
    points = half * cells_y
    columns = lax.axis_size("band")
    ring = columns // 2
    mine = lax.axis_index("band") // ring
    across = [(i, (i + ring) % columns) for i in range(columns)]

    sent = lax.dynamic_slice_in_dim(orbitals, half * (1 - mine), half, 0)
    kept = lax.dynamic_slice_in_dim(orbitals, half * mine, half, 0)
    came = lax.ppermute(sent, "band", across)
    both = jnp.stack([kept, came]).reshape(1, 2, points, lanes)
    groups = [list(range(ring)), list(range(ring, columns))]
    psi = lax.all_gather(both, "band", axis=0, tiled=True, axis_index_groups=groups)
    tall = spread(rotation, lax.ppermute(rotation, "band", across))
    out = rotate(tall, psi, (half, cells_y))
    keep, send, keep_x, send_x, keep_y, send_y = out

    ends = lax.axis_size("dx") - 1
    near, cross = [], []
    for x in range(ends):
        for i in range(ring):
            low, high = i, ring + i
            near += [(x * columns + high, (x + 1) * columns + high)]
            near += [((x + 1) * columns + low, x * columns + low)]
            cross += [(x * columns + high, (x + 1) * columns + low)]
            cross += [((x + 1) * columns + low, x * columns + high)]
    turn = [
        (y * columns + i, (1 - y) * columns + (i + ring) % columns)
        for y in range(2)
        for i in range(columns)
    ]
    keep_y = lax.ppermute(keep_y, "dy", [(0, 1), (1, 0)])
    send_y = lax.ppermute(send_y, ("dy", "band"), turn)
    got = lax.ppermute(send, "band", across)
    keep_x = lax.ppermute(keep_x, ("dx", "band"), near)
    send_x = lax.ppermute(send_x, ("dx", "band"), cross)
    shape = (half, cells_y, lanes)
    edge = (4, cells_y, lanes)
    rotated, applied = stencil(
        keep.reshape(shape), got.reshape(shape), keep_x.reshape(edge), send_x.reshape(edge),
        keep_y, send_y, potential,
    )
    return rotated, applied


def solution(mesh):
    return jax.shard_map(
        on_device,
        mesh=mesh,
        in_specs=(P("dx", "dy", "band"), P("band", None), P(None, "dx", "dy")),
        out_specs=(P("dx", "dy", "band"), P("dx", "dy", "band")),
        check_vma=False,
    )
```
